32 devices in a mesh: dp: 8 (over z, y), seq: 4 (over x, core).
Axes of the slice: x: 2, y: 2, z: 4, core: 2. Of those that a mesh axis runs over, the one named last changes fastest.
Arguments:
- tokens: bfloat16 [16384, 1024], P(('dp', 'seq')), may hold values from -6 to 6
- doc_starts: int32 [8, 4], P('dp'), may hold values from 0 to 2047, as said below
- routes: int32 [16384, 1], P(('dp', 'seq')), may hold values from 0 to 63; in each aligned block of 512 rows (0 to 511, 512 to 1023, ...) at most 16 rows name the same one
- ln1_gain: bfloat16 [1024], P('seq'), may hold values from 0.5 to 1.5
- ln1_bias: bfloat16 [1024], P('seq'), may hold values from -4 to 4
- w_qkv: bfloat16 [1024, 3072], P('seq'), may hold values from -0.1875 to 0.1875
- w_proj: bfloat16 [1024, 1024], P('seq'), may hold values from -0.75 to 0.75
- ln2_gain: bfloat16 [1024], P('seq'), may hold values from 0.5 to 1.5
- ln2_bias: bfloat16 [1024], P('seq'), may hold values from -4 to 4
- w_router: bfloat16 [1024, 64], P('seq'), may hold values from -0.09375 to 0.09375
- w_expert_in: bfloat16 [64, 1024, 4096], P('dp', None, 'seq'), may hold values from -0.1875 to 0.1875
- w_expert_out: bfloat16 [64, 4096, 1024], P('dp', 'seq'), may hold values from -12 to 12
- out_grad: bfloat16 [16384, 1024], P(('dp', 'seq')), may hold values from -6 to 6
Outputs:
- output: bfloat16 [16384, 1024], P(('dp', 'seq'))
- input_grad: float32 [16384, 1024], P(('dp', 'seq'))
- ln1_gain_grad: float32 [1024], P('seq')
- ln1_bias_grad: float32 [1024], P('seq')
- w_qkv_grad: float32 [1024, 3072], P('seq')
- w_proj_grad: float32 [1024, 1024], P('seq')
- ln2_gain_grad: float32 [1024], P('seq')
- ln2_bias_grad: float32 [1024], P('seq')
- w_router_grad: float32 [1024, 64], P('seq')
- w_expert_in_grad: float32 [64, 1024, 4096], P('dp', None, 'seq')
- w_expert_out_grad: float32 [64, 4096, 1024], P('dp', 'seq')
The draws below stay inside these ranges and needn't reach their ends.
Inputs may be any that keep to these rules, and one draw needn't show every extreme that they name: `doc_starts`: each row begins with 0 and rises strictly; entry j is where document j of sequence r begins. `routes`: among the 512 rows of one device (aligned blocks), no expert is named more than 16 times, a bound that some block reaches.
All inputs are finite; a program needn't handle non-finite values.
Results may differ from the reference program's by a relative error of at most 0.02.
Values may be sent and summed in bfloat16 or wider, within the bound.
A program may use at most 320 MiB of HBM per device.

```python
import math
import jax
import jax.numpy as jnp
import numpy as np
from jax import lax

D = 1024
H = 16
HD = 64
FF = 4096
EXPERTS = 64
TOK_DEV = 512
DOCS = 4
CAP = 16
SEQ_LEN = 2048
SEQS = 8
TOKENS = 16384
N_DP = 8
N_SEQ = 4


def draw_doc_starts(key, part):
    keys = jax.random.split(key, SEQS)
    row_ids = jnp.arange(SEQS, dtype=jnp.int32)

    def one_row(subkey, row_id):
        picks = jax.random.permutation(subkey, SEQ_LEN - 1)[:DOCS - 1] + 1
        ordered = jnp.sort(picks).astype(jnp.int32)
        last_pick = jnp.where(row_id == 0, jnp.int32(SEQ_LEN - 1), ordered[DOCS - 2])
        ordered = ordered.at[DOCS - 2].set(last_pick)
        return jnp.concatenate([jnp.zeros((1,), jnp.int32), ordered])
    return jax.vmap(one_row)(keys, row_ids)


def block_scale(key, shape, shards, low, high):
    factor_of, own = 1.0, jax.random.fold_in(key, 6)
    for dim, blocks in shards:
        steps = jnp.exp(jax.random.uniform(jax.random.fold_in(own, dim), (blocks,), jnp.float32, low / len(shards), high / len(shards)))
        factor_of = factor_of * jnp.repeat(steps, shape[dim] // blocks).reshape([-1 if axis == dim else 1 for axis in range(len(shape))])
    return factor_of


def deal_out(key, own, number, rows, count, top, bound, slope):
    order = jax.random.permutation(key, count)
    heavy_load, common = load_shares(count, rows * top, bound, slope, True), load_shares(count, rows * top, bound, slope, False)
    places = jnp.arange(count)

    def named(sizes, offset_by):
        used = int((sizes > 0).sum())
        fixed = max(1, used // 4)
        passed = fixed + (places - fixed + offset_by * (used - fixed)) % max(1, count - fixed)
        return jnp.zeros((count,), jnp.int32).at[order[jnp.where(places < fixed, places, passed)]].set(jnp.asarray(sizes, jnp.int32))

    sizes = jnp.where(number % 4 == 0, named(heavy_load, number // 4), named(common, number - number // 4 - 1))
    mixed = jax.random.permutation(jax.random.fold_in(own, 3), count)
    source_of, receiver = mixed[0:count // 2 * 2:2], mixed[1:count // 2 * 2:2]
    room = jnp.minimum(sizes[source_of] - 1, bound - sizes[receiver]) // 2
    room = jnp.where((source_of == order[0]) | (receiver == order[0]) | (sizes[receiver] == 0), 0, jnp.maximum(room, 0))
    passed = jax.random.randint(jax.random.fold_in(own, 4), (count // 2,), 0, 1 << 20) % (room + 1)
    sizes = sizes.at[source_of].add(-passed).at[receiver].add(passed)
    items = jnp.searchsorted(jnp.cumsum(sizes), jnp.arange(rows * top), side="right").astype(jnp.int32)
    listing = items.reshape(top, rows).T
    listing = listing[jax.random.permutation(jax.random.fold_in(own, 1), rows)]
    offset_by = jax.random.randint(jax.random.fold_in(own, 2), (rows, 1), 0, top)
    return jnp.take_along_axis(listing, (jnp.arange(top)[None, :] + offset_by) % top, axis=1)


def load_shares(number_of, total, bound, slope, full):
    portions = [(1 << 20) // math.isqrt(standing ** slope) + 1 for standing in range(1, number_of + 1)]
    largest = bound if full else min(bound, max(-(-total // number_of), total * portions[0] // sum(portions)))
    least = 1 if total - largest >= number_of - 1 else 0
    counts, surplus = [largest] + [least] * (number_of - 1), total - largest - least * (number_of - 1)
    while surplus > 0:
        candidates = [i for i in range(1, number_of) if counts[i] < largest] or [i for i in range(1, number_of) if counts[i] < bound]
        whole, left = sum([portions[i] for i in candidates]), surplus
        for i in candidates:
            more = min(bound - counts[i], max(1, left * portions[i] // whole), surplus)
            counts[i] = counts[i] + more
            surplus = surplus - more
    return np.array(counts)


def centred(own_key, extent, deviation, limit, shards=(), held_as=jnp.bfloat16):
    entries = deviation * jax.random.normal(own_key, extent, jnp.float32)
    if shards:
        entries = entries * block_scale(own_key, extent, shards, -0.22, 0.18)
    return jnp.clip(entries, -limit, limit).astype(held_as)


def setup_inputs(seed: int = 0) -> dict:
    arg_keys = jax.random.split(jax.random.key(seed), 14)
    tokens = centred(arg_keys[0], (TOKENS, D), 1.0, 6.0, ((0, 32),))
    doc_starts = draw_doc_starts(jax.random.fold_in(arg_keys[13], 71), 0)
    routes_keys = jax.random.split(jax.random.fold_in(arg_keys[2], 1), TOKENS // TOK_DEV)
    routes_turns = jax.random.permutation(jax.random.fold_in(arg_keys[2], 3), TOKENS // TOK_DEV)
    routes = jax.vmap(lambda own, number: deal_out(jax.random.fold_in(arg_keys[2], 2), own, number, TOK_DEV, EXPERTS, 1, CAP, 1))(routes_keys, routes_turns).reshape((TOKENS, 1))
    ln1_gain = jnp.clip(1.0 + 0.1 * jax.random.normal(arg_keys[3], (D,), jnp.float32), 0.5, 1.5).astype(jnp.bfloat16)
    ln1_bias = centred(arg_keys[4], (D,), 0.3, 4.0, ((0, 4),))
    w_qkv = centred(arg_keys[5], (D, 3 * D), D ** -0.5, 0.1875, ((0, 4),))
    w_proj = centred(arg_keys[6], (D, D), (D // 16) ** -0.5, 0.75, ((0, 4),))
    ln2_gain = jnp.clip(1.0 + 0.1 * jax.random.normal(arg_keys[7], (D,), jnp.float32), 0.5, 1.5).astype(jnp.bfloat16)
    ln2_bias = centred(arg_keys[8], (D,), 0.3, 4.0, ((0, 4),))
    w_router = centred(arg_keys[9], (D, EXPERTS), (4 * D) ** -0.5, 0.09375, ((0, 4),))
    w_expert_in = centred(arg_keys[10], (EXPERTS, D, FF), D ** -0.5, 0.1875, ((0, 8), (2, 4)))
    w_expert_out = centred(arg_keys[11], (EXPERTS, FF, D), (2.0 * EXPERTS / FF ** 0.5), 12.0, ((0, 8), (1, 4)))
    out_grad = centred(arg_keys[12], (TOKENS, D), 1.0, 6.0, ((0, 32),))
    return {"tokens": tokens, "doc_starts": doc_starts, "routes": routes, "ln1_gain": ln1_gain, "ln1_bias": ln1_bias, "w_qkv": w_qkv, "w_proj": w_proj, "ln2_gain": ln2_gain, "ln2_bias": ln2_bias, "w_router": w_router, "w_expert_in": w_expert_in, "w_expert_out": w_expert_out, "out_grad": out_grad}


EPS = 1e-05
NEG = -1e+30

@jax.custom_vjp
def low(v):
    return lax.optimization_barrier(v.astype(jnp.bfloat16)).astype(jnp.float32)

@jax.custom_vjp
def low_back(v):
    return v

def low_keep(v):
    return (low(v), None)

def low_pass(kept, grad):
    return (grad,)

def back_keep(v):
    return (v, None)

def back_low(kept, grad):
    return (low(grad),)
low.defvjp(low_keep, low_pass)
low_back.defvjp(back_keep, back_low)

def matmul(left, right):
    return jnp.dot(left, right, precision=lax.Precision.HIGHEST)

def layer_norm(values, gain, shift):
    center = values - lax.optimization_barrier(jnp.mean(values, axis=-1, keepdims=True))
    spread = lax.optimization_barrier(jnp.mean(center * center, axis=-1, keepdims=True))
    return center * lax.rsqrt(spread + EPS) * gain + shift

def attend(packed):
    qkv_seq, starts = packed
    factor = HD ** (-0.5)
    queries = qkv_seq[:, 0]
    key_rows = qkv_seq[:, 1]
    value_rows = qkv_seq[:, 2]
    position = jnp.arange(SEQ_LEN, dtype=jnp.int32)
    doc_first = lax.optimization_barrier(jnp.max(jnp.where(starts[None, :] <= position[:, None], starts[None, :], 0), axis=1))
    allowed = (position[None, :] <= position[:, None]) & (position[None, :] >= doc_first[:, None])
    scores = low_back(jnp.einsum('qhd,khd->hqk', queries, key_rows, precision=lax.Precision.HIGHEST) * factor)
    scores = jnp.where(allowed[None], scores, NEG)
    row_top = lax.optimization_barrier(jnp.max(scores, axis=-1, keepdims=True))
    weights = jnp.exp(scores - row_top)
    probs = weights / lax.optimization_barrier(jnp.sum(weights, axis=-1, keepdims=True))
    return jnp.einsum('hqk,khd->qhd', low(probs), value_rows, precision=lax.Precision.HIGHEST)

def expert_apply(packed):
    rows_in, first_weight, second_weight = packed
    pre_act = low_back(matmul(rows_in, first_weight))
    hidden = low(jax.nn.gelu(pre_act))
    return matmul(hidden, second_weight)

def reference(tokens, doc_starts, routes, ln1_gain, ln1_bias, w_qkv, w_proj, ln2_gain, ln2_bias, w_router, w_expert_in, w_expert_out, out_grad):
    blocks = N_DP * N_SEQ
    expert_ids = routes[:, 0].astype(jnp.int32)
    block_choice = expert_ids.reshape(blocks, TOK_DEV)
    expert_range = jnp.arange(EXPERTS, dtype=jnp.int32)
    onehot_int = (block_choice[:, :, None] == expert_range[None, None, :]).astype(jnp.int32)
    ranking = lax.optimization_barrier(jnp.sum((jnp.cumsum(onehot_int, axis=1) - 1) * onehot_int, axis=2))
    block_ids = jnp.arange(blocks, dtype=jnp.int32)[:, None]
    token_slot = ((block_ids * EXPERTS + block_choice) * CAP + ranking).reshape(-1).astype(jnp.int32)
    slot_token = jnp.zeros((blocks * EXPERTS * CAP,), jnp.int32).at[token_slot].set(jnp.arange(TOKENS, dtype=jnp.int32))
    selector = (expert_ids[:, None] == expert_range[None, :]).astype(jnp.float32)

    def forward(inputs, gain_one, bias_one, qkv_weight, proj_weight, gain_two, bias_two, router_weight, first_weight, second_weight):
        normed = low(layer_norm(inputs, gain_one, bias_one))
        qkv = low_back(low(matmul(normed, qkv_weight)))
        packed = qkv.reshape(SEQS, SEQ_LEN, 3, H, HD)
        attended = lax.map(jax.checkpoint(attend), (packed, doc_starts))
        heads_out = low_back(low(attended.reshape(TOKENS, D)))
        middle = inputs + low_back(matmul(heads_out, proj_weight))
        normed_two = low(layer_norm(middle, gain_two, bias_two))
        logits = matmul(normed_two, router_weight)
        row_top = lax.optimization_barrier(jnp.max(logits, axis=-1, keepdims=True))
        weights = jnp.exp(logits - row_top)
        probs = weights / lax.optimization_barrier(jnp.sum(weights, axis=-1, keepdims=True))
        gate = lax.optimization_barrier(jnp.sum(probs * selector, axis=1))
        expert_in = low_back(normed_two)
        gathered = expert_in[slot_token].reshape(blocks, EXPERTS, CAP, D)
        gathered = gathered.transpose(1, 0, 2, 3).reshape(EXPERTS, blocks * CAP, D)
        produced = lax.map(jax.checkpoint(expert_apply), (gathered, first_weight, second_weight))
        produced = low_back(low(produced))
        produced = produced.reshape(EXPERTS, blocks, CAP, D).transpose(1, 0, 2, 3).reshape(blocks * EXPERTS * CAP, D)
        return middle + gate[:, None] * produced[token_slot]
    output, pull = jax.vjp(forward, tokens.astype(jnp.float32), ln1_gain.astype(jnp.float32), ln1_bias.astype(jnp.float32), w_qkv.astype(jnp.float32), w_proj.astype(jnp.float32), ln2_gain.astype(jnp.float32), ln2_bias.astype(jnp.float32), w_router.astype(jnp.float32), w_expert_in.astype(jnp.float32), w_expert_out.astype(jnp.float32))
    grads = pull(out_grad.astype(jnp.float32))
    return (output.astype(jnp.bfloat16), grads[0], grads[1], grads[2], grads[3], grads[4], grads[5], grads[6], grads[7], grads[8], grads[9])
```

```python
import functools
import jax
import jax.numpy as jnp
from jax import lax
from jax.experimental import pallas as pl
from jax.experimental.pallas import tpu as pltpu
from jax.sharding import PartitionSpec as P

HD = 64
NEG = -1e30


def _contract(left, right, dims):
    return lax.dot_general(left, right, ((dims[0:1], dims[1:2]), ((), ())), preferred_element_type=jnp.float32)


def _lanes(block, odd):
    lane = lax.broadcasted_iota(jnp.int32, block.shape, 1)
    keep = (lane >= HD) if odd else (lane < HD)
    return jnp.where(keep, block, jnp.zeros_like(block))


def attend_kernel(lows, qkv_ref, first_ref, out_ref, lse_ref, *, rows, keys, width, span):
    index = pl.program_id(0)
    begin = index * rows
    first = first_ref[:, pl.ds(pl.multiple_of(begin, rows), rows)]
    reach = begin + lax.broadcasted_iota(jnp.int32, (1, rows), 1) - first
    low = lows[index]
    high = (begin + rows + keys - 1) // keys
    begin = pl.multiple_of(begin, rows)
    for group in range(width // 128 // span):
        heads = [(group * span + i // 2, i % 2) for i in range(2 * span)]
        queries = [
            _lanes(qkv_ref[pl.ds(begin, rows), pair * 128 : pair * 128 + 128], odd) * (HD ** (-0.5))
            for pair, odd in heads
        ]

        def step(block, carry):
            start = pl.multiple_of(block * keys, keys)
            offset = start + lax.broadcasted_iota(jnp.int32, (keys, rows), 0) - first
            allowed = (offset >= 0) & (offset <= reach)
            fresh = []
            for (pair, odd), q_head, (top, total, acc) in zip(heads, queries, carry):
                column = pair * 128
                k_block = qkv_ref[pl.ds(start, keys), width + column : width + column + 128]
                v_block = qkv_ref[pl.ds(start, keys), 2 * width + column : 2 * width + column + 128]
                scores = jnp.where(allowed, _contract(k_block, q_head, (1, 1)), NEG)
                new_top = jnp.maximum(top, jnp.max(scores, axis=0, keepdims=True))
                weights = jnp.exp(scores - new_top)
                shrink = jnp.exp(top - new_top)
                total = total * shrink + jnp.sum(weights, axis=0, keepdims=True)
                acc = acc * shrink + _contract(v_block, weights.astype(jnp.bfloat16), (0, 0))
                fresh.append((new_top, total, acc))
            return fresh

        done = lax.fori_loop(
            low,
            high,
            step,
            [
                (
                    jnp.full((1, rows), NEG, jnp.float32),
                    jnp.zeros((1, rows), jnp.float32),
                    jnp.zeros((128, rows), jnp.float32),
                )
                for _ in heads
            ],
        )
        halves = []
        for (pair, odd), (top, total, acc) in zip(heads, done):
            lse_ref[2 * pair + odd, :, :] = top + jnp.log(total)
            halves.append((acc * (1.0 / total))[odd * HD : (odd + 1) * HD])
        joined = jnp.concatenate(halves, axis=0)
        out_ref[:, group * span * 128 : (group + 1) * span * 128] = joined.T.astype(jnp.bfloat16)


def attend(qkv, first, lows, rows, keys, span=2):
    length, width = qkv.shape[0], qkv.shape[1] // 3
    heads = width // HD
    return pl.pallas_call(
        functools.partial(attend_kernel, rows=rows, keys=keys, width=width, span=span),
        grid_spec=pltpu.PrefetchScalarGridSpec(
            num_scalar_prefetch=1,
            grid=(length // rows,),
            in_specs=[
                pl.BlockSpec((length, 3 * width), lambda i, lows: (0, 0)),
                pl.BlockSpec((1, length), lambda i, lows: (0, 0)),
            ],
            out_specs=[
                pl.BlockSpec((rows, width), lambda i, lows: (i, 0)),
                pl.BlockSpec((heads, 1, rows), lambda i, lows: (0, 0, i)),
            ],
        ),
        out_shape=[
            jax.ShapeDtypeStruct((length, width), jnp.bfloat16),
            jax.ShapeDtypeStruct((heads, 1, length), jnp.float32),
        ],
        compiler_params=pltpu.CompilerParams(vmem_limit_bytes=48 << 20),
        cost_estimate=pl.CostEstimate(
            flops=2 * heads * length * length * 128, bytes_accessed=8 * length * width, transcendentals=heads * length * length // 2
        ),
        name="attend",
    )(lows, qkv, first)


def attend_back_kernel(
    lows, qkv_ref, first_ref, lse_ref, out_ref, grad_ref, dqkv_ref, dk_acc, dv_acc, *, rows, keys, width, span
):
    index = pl.program_id(0)
    length = qkv_ref.shape[0]

    @pl.when(index == 0)
    def _():
        dk_acc[...] = jnp.zeros_like(dk_acc)
        dv_acc[...] = jnp.zeros_like(dv_acc)

    begin = pl.multiple_of(index * rows, rows)
    first = first_ref[:, pl.ds(begin, rows)]
    reach = begin + lax.broadcasted_iota(jnp.int32, (1, rows), 1) - first
    low = lows[index]
    high = (begin + rows + keys - 1) // keys
    for group in range(width // 128 // span):
        heads = [(group * span + i // 2, i % 2) for i in range(2 * span)]
        fixed = []
        for pair, odd in heads:
            columns = slice(pair * 128, pair * 128 + 128)
            g_pair = grad_ref[pl.ds(begin, rows), columns]
            o_pair = out_ref[pl.ds(begin, rows), columns]
            products = _lanes(g_pair.astype(jnp.float32) * o_pair.astype(jnp.float32), odd).T
            fixed.append(
                (
                    _lanes(qkv_ref[pl.ds(begin, rows), columns], odd) * (HD ** (-0.5)),
                    _lanes(g_pair, odd),
                    lse_ref[2 * pair + odd, :, pl.ds(begin, rows)],
                    jnp.sum(products, axis=0, keepdims=True),
                )
            )

        def step(block, carry):
            start = pl.multiple_of(block * keys, keys)
            offset = start + lax.broadcasted_iota(jnp.int32, (keys, rows), 0) - first
            allowed = (offset >= 0) & (offset <= reach)
            fresh = []
            for (pair, odd), (q_head, g_head, lse, row_dot), dq in zip(heads, fixed, carry):
                column = pair * 128
                k_block = qkv_ref[pl.ds(start, keys), width + column : width + column + 128]
                v_block = qkv_ref[pl.ds(start, keys), 2 * width + column : 2 * width + column + 128]
                scores = jnp.where(allowed, _contract(k_block, q_head, (1, 1)), NEG)
                weights = jnp.exp(scores - lse)
                grad_weights = _contract(v_block, g_head, (1, 1))
                grad_scores = (weights * (grad_weights - row_dot)).astype(jnp.bfloat16)
                dv_acc[pl.ds(start, keys), column : column + 128] += _contract(
                    weights.astype(jnp.bfloat16), g_head, (1, 0)
                )
                dk_acc[pl.ds(start, keys), column : column + 128] += _contract(grad_scores, q_head, (1, 0))
                fresh.append(dq + _contract(k_block, grad_scores, (0, 0)))
            return fresh

        done = lax.fori_loop(low, high, step, [jnp.zeros((128, rows), jnp.float32) for _ in heads])
        joined = jnp.concatenate(
            [dq[odd * HD : (odd + 1) * HD] for (_, odd), dq in zip(heads, done)], axis=0
        ) * (HD ** (-0.5))
        dqkv_ref[pl.ds(begin, rows), group * span * 128 : (group + 1) * span * 128] = joined.T.astype(jnp.bfloat16)

    @pl.when(index == pl.num_programs(0) - 1)
    def _():
        dqkv_ref[:, width : 2 * width] = dk_acc[...].astype(jnp.bfloat16)
        dqkv_ref[:, 2 * width :] = dv_acc[...].astype(jnp.bfloat16)


def attend_back(qkv, first, lse, out, grad, lows, rows, keys, span=2):
    length, width = qkv.shape[0], qkv.shape[1] // 3
    heads = width // HD
    whole = lambda shape: pl.BlockSpec(shape, lambda i, lows: (0,) * len(shape))
    return pl.pallas_call(
        functools.partial(attend_back_kernel, rows=rows, keys=keys, width=width, span=span),
        grid_spec=pltpu.PrefetchScalarGridSpec(
            num_scalar_prefetch=1,
            grid=(length // rows,),
            in_specs=[
                whole((length, 3 * width)),
                whole((1, length)),
                whole((heads, 1, length)),
                whole((length, width)),
                whole((length, width)),
            ],
            out_specs=whole((length, 3 * width)),
            scratch_shapes=[pltpu.VMEM((length, width), jnp.float32)] * 2,
        ),
        out_shape=jax.ShapeDtypeStruct((length, 3 * width), jnp.bfloat16),
        compiler_params=pltpu.CompilerParams(vmem_limit_bytes=56 << 20),
        cost_estimate=pl.CostEstimate(
            flops=5 * heads * length * length * 128, bytes_accessed=18 * length * width, transcendentals=heads * length * length // 2
        ),
        name="attend_back",
    )(lows, qkv, first, lse, out, grad)


EXPERTS = 64
MESH = pl.DeviceIdType.MESH


def moe_kernel(
    send_ref,
    router_ref,
    win_ref,
    wout_ref,
    back_ref,
    rows_out,
    scaled_out,
    hidden_out,
    dpre_out,
    held,
    near,
    far,
    parts,
    relay,
    own,
    final,
    win_buf,
    wout_buf,
    scaled_buf,
    hidden_buf,
    dpre_buf,
    disp_send,
    disp_recv,
    core_send,
    core_recv,
    pair_send,
    pair_recv,
    pass_send,
    pass_recv,
    half_send,
    half_recv,
    rest_send,
    rest_recv,
    back_send,
    back_recv,
    load_sem,
    store_sem,
    rows_sem,
    local_sem,
    *,
    dp_count,
    seq_count,
    local,
    cap,
    group,
    tile,
):
    chunks = local * (dp_count // group)
    parts_of = dp_count // group
    me, my_seq = lax.axis_index("dp"), lax.axis_index("seq")
    my_part = me // group
    lane = me % group
    mate, pair = my_seq + 1 - 2 * (my_seq % 2), (my_seq + 2) % 4
    block = group * cap
    total = seq_count * block
    depth = send_ref.shape[3] // 2
    inner = win_ref.shape[2]

    barrier = pltpu.get_barrier_semaphore()

    def greet(k, _):
        pl.semaphore_signal(barrier, inc=1, device_id=((me + k) % dp_count, my_seq), device_id_type=MESH)
        return 0

    lax.fori_loop(1, dp_count, greet, 0)
    pl.semaphore_signal(barrier, inc=1, device_id=(me, mate), device_id_type=MESH)
    pl.semaphore_signal(barrier, inc=1, device_id=(me, pair), device_id_type=MESH)

    def block_of(seq):
        return pl.ds(pl.multiple_of(seq * block, block), block)

    def load(chunk):
        slot = chunk % 2
        expert = chunk // parts_of
        return (
            pltpu.make_async_copy(win_ref.at[expert], win_buf.at[slot], load_sem.at[slot, 0]),
            pltpu.make_async_copy(wout_ref.at[expert], wout_buf.at[slot], load_sem.at[slot, 1]),
        )

    def dispatch(expert, peer):
        chunk = expert * parts_of + my_part
        place = pl.ds(pl.multiple_of(my_seq * block + lane * cap, cap), cap)
        return pltpu.make_async_remote_copy(
            src_ref=send_ref.at[peer, expert],
            dst_ref=held.at[chunk, place],
            send_sem=disp_send.at[chunk],
            recv_sem=disp_recv.at[chunk],
            device_id=(peer, my_seq),
            device_id_type=MESH,
        )

    def start_dispatch(chunk):
        @pl.when(chunk % parts_of == my_part)
        def _():
            expert = chunk // parts_of
            place = pl.ds(pl.multiple_of(my_seq * block + lane * cap, cap), cap)
            pltpu.make_async_copy(
                send_ref.at[me, expert], held.at[chunk, place], disp_recv.at[chunk]
            ).start()

            def one(k, _):
                dispatch(expert, (me + k) % dp_count).start()
                return 0

            lax.fori_loop(1, dp_count, one, 0)

    def wait_bytes(ref, sem):
        pltpu.make_async_copy(ref, ref, sem).wait()

    def gather_copy(chunk, seq, target, send_sem, recv_sem):
        return pltpu.make_async_remote_copy(
            src_ref=held.at[chunk, block_of(seq)],
            dst_ref=held.at[chunk, block_of(seq)],
            send_sem=send_sem.at[chunk],
            recv_sem=recv_sem.at[chunk],
            device_id=(me, target),
            device_id_type=MESH,
        )

    def start_gather(chunk):
        wait_bytes(held.at[chunk, block_of(my_seq)], disp_recv.at[chunk])
        gather_copy(chunk, my_seq, pair, pair_send, pair_recv).start()
        gather_copy(chunk, my_seq, mate, core_send, core_recv).start()

    def start_pass(chunk):
        gather_copy(chunk, my_seq, pair, pair_send, pair_recv).wait_recv()
        gather_copy(chunk, pair, mate, pass_send, pass_recv).start()

    def half_copy(chunk, side):
        return pltpu.make_async_remote_copy(
            src_ref=parts.at[chunk % 2, block_of(2 * side + mate % 2)],
            dst_ref=near.at[chunk, side],
            send_sem=half_send.at[chunk, side],
            recv_sem=half_recv.at[chunk, side],
            device_id=(me, mate),
            device_id_type=MESH,
        )

    def rest_copy(chunk):
        return pltpu.make_async_remote_copy(
            src_ref=relay.at[chunk % 2],
            dst_ref=far.at[chunk],
            send_sem=rest_send.at[chunk],
            recv_sem=rest_recv.at[chunk],
            device_id=(me, pair),
            device_id_type=MESH,
        )

    def back_copy(chunk, peer):
        expert = chunk // parts_of
        return pltpu.make_async_remote_copy(
            src_ref=final.at[chunk % 2, pl.ds(pl.multiple_of((peer % group) * cap, cap), cap)],
            dst_ref=back_ref.at[me, expert],
            send_sem=back_send.at[chunk],
            recv_sem=back_recv.at[expert],
            device_id=(peer, my_seq),
            device_id_type=MESH,
        )

    def back_local(chunk):
        expert = chunk // parts_of
        return pltpu.make_async_copy(
            final.at[chunk % 2, pl.ds(pl.multiple_of(lane * cap, cap), cap)],
            back_ref.at[me, expert],
            local_sem.at[chunk % 2],
        )

    def rows_copy(chunk):
        return pltpu.make_async_copy(held.at[chunk, :, pl.ds(0, depth)], rows_out.at[chunk], rows_sem.at[chunk])

    def stores(chunk):
        slot = chunk % 2
        return (
            pltpu.make_async_copy(scaled_buf.at[slot], scaled_out.at[chunk], store_sem.at[slot, 0]),
            pltpu.make_async_copy(hidden_buf.at[slot], hidden_out.at[chunk], store_sem.at[slot, 1]),
            pltpu.make_async_copy(dpre_buf.at[slot], dpre_out.at[chunk], store_sem.at[slot, 2]),
        )

    def compute(chunk):
        slot = chunk % 2
        expert = me * local + chunk // parts_of
        gather_copy(chunk, my_seq, mate, core_send, core_recv).wait_recv()
        gather_copy(chunk, pair, mate, pass_send, pass_recv).wait_recv()
        rows_copy(chunk).start()
        rows = held[chunk, :, 0:depth]
        logits = jnp.dot(rows, router_ref[...], preferred_element_type=jnp.float32)
        lanes = lax.broadcasted_iota(jnp.int32, logits.shape, 1)
        logits = jnp.where(lanes < EXPERTS, logits, NEG)
        weights = jnp.exp(logits - jnp.max(logits, axis=1, keepdims=True))
        chosen = jnp.sum(jnp.where(lanes == expert, weights, 0.0), axis=1, keepdims=True)
        gate = chosen / jnp.sum(weights, axis=1, keepdims=True)

        @pl.when(chunk >= 2)
        def _():
            for copy in stores(chunk - 2):
                copy.wait()

        scaled_buf[slot] = (held[chunk, :, depth : 2 * depth].astype(jnp.float32) * gate).astype(jnp.bfloat16)
        for copy in load(chunk):
            copy.wait()

        def first(index, _):
            columns = pl.ds(pl.multiple_of(index * tile, tile), tile)
            pre = jnp.dot(held[chunk, :, 0:depth], win_buf[slot, :, columns], preferred_element_type=jnp.float32)
            back = lax.dot_general(
                scaled_buf[slot],
                wout_buf[slot, columns, :],
                (((1,), (1,)), ((), ())),
                preferred_element_type=jnp.float32,
            )
            root = 0.7978845608028654
            square = pre * pre
            curve = jnp.tanh(root * pre * (1.0 + 0.044715 * square))
            upper = 0.5 * (1.0 + curve)
            slope = upper + (0.5 * root) * pre * (1.0 - curve * curve) * (1.0 + (3 * 0.044715) * square)
            hidden_buf[slot, :, columns] = (pre * upper).astype(jnp.bfloat16)
            dpre_buf[slot, :, columns] = (back * slope).astype(jnp.bfloat16)
            return 0

        lax.fori_loop(0, inner // tile, first, 0)
        for copy in stores(chunk):
            copy.start()

        def second(index, _):
            columns = pl.ds(pl.multiple_of(index * tile, tile), tile)
            parts[slot, :, columns] = jnp.dot(
                hidden_buf[slot], wout_buf[slot, :, columns], preferred_element_type=jnp.float32
            ).astype(jnp.bfloat16)
            others = pl.ds(pl.multiple_of(depth + index * tile, tile), tile)
            parts[slot, :, others] = lax.dot_general(
                dpre_buf[slot],
                win_buf[slot, columns, :],
                (((1,), (1,)), ((), ())),
                preferred_element_type=jnp.float32,
            ).astype(jnp.bfloat16)
            return 0

        lax.fori_loop(0, depth // tile, second, 0)
        for side in range(2):
            half_copy(chunk, side).start()

    def start_rest(chunk):
        slot = chunk % 2
        for side in range(2):
            half_copy(chunk, side).wait()
        far_side, my_side = pair // 2, my_seq // 2

        @pl.when(chunk >= 2)
        def _():
            rest_copy(chunk - 2).wait_send()

        relay[slot] = (
            parts[slot, block_of(pair)].astype(jnp.float32) + near[chunk, far_side].astype(jnp.float32)
        ).astype(jnp.bfloat16)
        rest_copy(chunk).start()
        own[slot] = parts[slot, block_of(my_seq)].astype(jnp.float32) + near[chunk, my_side].astype(jnp.float32)

    def wait_back(chunk):
        @pl.when(chunk % parts_of == my_part)
        def _():
            wait_bytes(final.at[0, pl.ds(0, (group - 1) * cap)], back_send.at[chunk])
            back_local(chunk).wait()

        @pl.when(chunk % parts_of != my_part)
        def _():
            wait_bytes(final.at[0], back_send.at[chunk])

    def start_back(chunk):
        slot = chunk % 2
        part = chunk % parts_of
        rest_copy(chunk).wait_recv()

        @pl.when(chunk >= 2)
        def _():
            wait_back(chunk - 2)

        final[slot] = (own[slot] + far[chunk].astype(jnp.float32)).astype(jnp.bfloat16)

        def one(k, _):
            peer = part * group + (lane + k) % group

            @pl.when(peer == me)
            def _():
                back_local(chunk).start()

            @pl.when(peer != me)
            def _():
                back_copy(chunk, peer).start()

            return 0

        lax.fori_loop(0, group, one, 0)

    for copy in load(0):
        copy.start()
    pl.semaphore_wait(barrier, dp_count + 1)

    def step(time, _):
        @pl.when(time < chunks)
        def _():
            start_dispatch(time)

        @pl.when((time >= 1) & (time < chunks + 1))
        def _():
            start_gather(time - 1)

        @pl.when((time >= 2) & (time < chunks + 2))
        def _():
            start_pass(time - 2)

        @pl.when((time >= 4) & (time < chunks + 4))
        def _():
            start_rest(time - 4)

        @pl.when((time >= 5) & (time < chunks + 5))
        def _():
            start_back(time - 5)

        @pl.when((time >= 3) & (time < chunks + 3))
        def _():
            chunk = time - 3

            @pl.when(chunk + 1 < chunks)
            def _():
                for copy in load(chunk + 1):
                    copy.start()

            compute(chunk)

        return 0

    lax.fori_loop(0, chunks + 5, step, 0)

    def drain(chunk, _):
        @pl.when(chunk % parts_of == my_part)
        def _():
            wait_bytes(send_ref.at[pl.ds(0, dp_count - 1), 0], disp_send.at[chunk])

        gather_copy(chunk, my_seq, pair, pair_send, pair_recv).wait_send()
        gather_copy(chunk, my_seq, mate, core_send, core_recv).wait_send()
        gather_copy(chunk, pair, mate, pass_send, pass_recv).wait_send()
        rows_copy(chunk).wait()

        @pl.when(chunk >= chunks - 2)
        def _():
            for copy in stores(chunk):
                copy.wait()
            rest_copy(chunk).wait_send()
            wait_back(chunk)

        return 0

    lax.fori_loop(0, chunks, drain, 0)

    def arrive(expert, _):
        wait_bytes(back_ref.at[pl.ds(0, dp_count - 1), expert], back_recv.at[expert])
        return 0

    lax.fori_loop(0, local, arrive, 0)


def experts_exchange(send, router, w_in, w_out):
    dp_count, local, cap, width = send.shape
    width = width // 2
    inner = w_in.shape[2]
    seq_count = lax.axis_size("seq")
    group = min(8, dp_count)
    chunks = local * (dp_count // group)
    block = group * cap
    total = seq_count * block
    tile = 256
    bf = jnp.bfloat16
    anywhere = pl.BlockSpec(memory_space=pl.ANY)
    dma = pltpu.SemaphoreType.DMA
    flops = 2 * 4 * chunks * total * width * inner
    return pl.pallas_call(
        functools.partial(
            moe_kernel, dp_count=dp_count, seq_count=seq_count, local=local, cap=cap, group=group, tile=tile
        ),
        in_specs=[anywhere, pl.BlockSpec(memory_space=pltpu.VMEM), anywhere, anywhere],
        out_specs=[anywhere] * 5,
        out_shape=[
            jax.ShapeDtypeStruct(send.shape, bf),
            jax.ShapeDtypeStruct((chunks, total, width), bf),
            jax.ShapeDtypeStruct((chunks, total, width), bf),
            jax.ShapeDtypeStruct((chunks, total, inner), bf),
            jax.ShapeDtypeStruct((chunks, total, inner), bf),
        ],
        scratch_shapes=[
            pltpu.VMEM((chunks, total, 2 * width), bf),
            pltpu.VMEM((chunks, 2, block, 2 * width), bf),
            pltpu.VMEM((chunks, block, 2 * width), bf),
            pltpu.VMEM((2, total, 2 * width), bf),
            pltpu.VMEM((2, block, 2 * width), bf),
            pltpu.VMEM((2, block, 2 * width), jnp.float32),
            pltpu.VMEM((2, block, 2 * width), bf),
            pltpu.VMEM((2, width, inner), bf),
            pltpu.VMEM((2, inner, width), bf),
            pltpu.VMEM((2, total, width), bf),
            pltpu.VMEM((2, total, inner), bf),
            pltpu.VMEM((2, total, inner), bf),
            dma((chunks,)),
            dma((chunks,)),
            dma((chunks,)),
            dma((chunks,)),
            dma((chunks,)),
            dma((chunks,)),
            dma((chunks,)),
            dma((chunks,)),
            dma((chunks, 2)),
            dma((chunks, 2)),
            dma((chunks,)),
            dma((chunks,)),
            dma((chunks,)),
            dma((local,)),
            dma((2, 2)),
            dma((2, 3)),
            dma((chunks,)),
            dma((2,)),
        ],
        compiler_params=pltpu.CompilerParams(
            collective_id=1, has_side_effects=True, vmem_limit_bytes=62 << 20
        ),
        cost_estimate=pl.CostEstimate(flops=flops, bytes_accessed=96 << 20, transcendentals=0),
        name="experts",
    )(send, router, w_in, w_out)


H = 16
EPS = 1e-05
PACK_ROWS = 80


def normalize(values):
    center = values - jnp.mean(values, axis=-1, keepdims=True)
    inverse = lax.rsqrt(jnp.mean(center * center, axis=-1, keepdims=True) + EPS)
    return (center * inverse, inverse)


def norm_back(grad_norm, normed, inverse):
    first_mean = jnp.mean(grad_norm, axis=-1, keepdims=True)
    second_mean = jnp.mean(grad_norm * normed, axis=-1, keepdims=True)
    return inverse * (grad_norm - first_mean - normed * second_mean)


def dot(left, right, dims):
    return lax.dot_general(left, right, ((dims[0:1], dims[1:2]), ((), ())), preferred_element_type=jnp.float32)


def per_device(
    tokens,
    doc_starts,
    routes,
    ln1_gain,
    ln1_bias,
    w_qkv,
    w_proj,
    ln2_gain,
    ln2_bias,
    w_router,
    w_expert_in,
    w_expert_out,
    out_grad,
):
    seq_count = lax.axis_size("seq")
    dp_count = lax.axis_size("dp")
    seq_index = lax.axis_index("seq")
    row_count, width = tokens.shape
    length = row_count * seq_count
    shard = width // seq_count
    head_width = H // seq_count * HD
    local_experts = EXPERTS // dp_count
    capacity = max(2, 2 * row_count // EXPERTS)

    expert_ids = routes[:, 0]
    selector = expert_ids[:, None] == jnp.arange(EXPERTS, dtype=jnp.int32)[None, :]
    selector_float = selector.astype(jnp.float32)
    row_range = jnp.arange(row_count, dtype=jnp.int32)
    earlier = (row_range[:, None] > row_range[None, :]).astype(jnp.bfloat16)
    counts = jnp.dot(earlier, selector.astype(jnp.bfloat16), preferred_element_type=jnp.float32)
    ranking = jnp.sum(counts * selector_float, axis=1).astype(jnp.int32)
    slot_ids = expert_ids * capacity + ranking
    placement = (
        jnp.arange(EXPERTS * capacity, dtype=jnp.int32)[:, None] == slot_ids[None, :]
    ).astype(jnp.bfloat16)

    small = jnp.concatenate(
        [
            w_router.T,
            jnp.stack([ln1_gain, ln1_bias, ln2_gain, ln2_bias]),
            jnp.zeros((PACK_ROWS - EXPERTS - 4, shard), jnp.bfloat16),
        ],
        axis=0,
    )
    small_all = lax.all_gather(small, "seq", axis=1, tiled=True)
    router_weight = small_all[:EXPERTS].T
    gains = small_all[EXPERTS : EXPERTS + 4].astype(jnp.float32)
    gain_one, bias_one, gain_two, bias_two = gains[0], gains[1], gains[2], gains[3]
    tokens_all = lax.all_gather(tokens, "seq", axis=0, tiled=True)
    qkv_pieces = w_qkv.reshape(shard, 3, seq_count, head_width).transpose(2, 0, 1, 3)
    qkv_weight = lax.all_to_all(
        qkv_pieces.reshape(seq_count, shard, 3 * head_width), "seq", split_axis=0, concat_axis=0, tiled=True
    ).reshape(width, 3 * head_width)
    proj_weight = lax.all_gather(w_proj, "seq", axis=0, tiled=True)
    normed_all, _ = normalize(tokens_all.astype(jnp.float32))
    hidden_all = (normed_all * gain_one + bias_one).astype(jnp.bfloat16)
    qkv = dot(hidden_all, qkv_weight, (1, 0)).astype(jnp.bfloat16)

    starts = doc_starts[0]
    positions = jnp.arange(length, dtype=jnp.int32)
    doc_first = jnp.max(jnp.where(starts[None, :] <= positions[:, None], starts[None, :], 0), axis=1)
    block = min(512, length)
    lows = doc_first[::block] // block
    heads_out, lse = attend(qkv, doc_first[None, :], lows, block, block)
    token_heads = lax.all_to_all(
        heads_out.reshape(seq_count, row_count, head_width), "seq", split_axis=0, concat_axis=0, tiled=True
    )
    token_heads = token_heads.transpose(1, 0, 2).reshape(row_count, width)

    inputs = tokens.astype(jnp.float32)
    middle = inputs + dot(token_heads, proj_weight, (1, 0))
    normed_two, inverse_two = normalize(middle)
    hidden_two = (normed_two * gain_two + bias_two).astype(jnp.bfloat16)
    both = jnp.concatenate([hidden_two, out_grad], axis=1)
    send = dot(placement, both, (1, 0)).astype(jnp.bfloat16)
    send = send.reshape(dp_count, local_experts, capacity, 2 * width)
    router_wide = jnp.pad(router_weight, ((0, 0), (0, 128 - EXPERTS)))
    back, rows_in, scaled, hidden, grad_pre = experts_exchange(send, router_wide, w_expert_in, w_expert_out)
    logits = dot(hidden_two, router_weight, (1, 0))
    probs = jax.nn.softmax(logits, axis=-1)
    gate = jnp.sum(probs * selector_float, axis=1)
    grad_out = out_grad.astype(jnp.float32)

    by_expert = lambda values: values.reshape(local_experts, -1, values.shape[2])
    expert_in_grad = jnp.einsum(
        "erd,erf->edf", by_expert(rows_in), by_expert(grad_pre), preferred_element_type=jnp.float32
    )
    expert_out_grad = jnp.einsum(
        "erf,erd->efd", by_expert(hidden), by_expert(scaled), preferred_element_type=jnp.float32
    )
    combined = dot(placement, back.reshape(EXPERTS * capacity, 2 * width), (0, 0))
    expert_out, expert_dx = combined[:, :width], combined[:, width:]
    output = (middle + gate[:, None] * expert_out).astype(jnp.bfloat16)
    grad_gate = jnp.sum(grad_out * expert_out, axis=1)
    grad_logits = probs * (selector_float - gate[:, None]) * grad_gate[:, None]
    router_grad = lax.dot_general(
        grad_logits,
        hidden_two.astype(jnp.float32),
        (((0,), (0,)), ((), ())),
        precision=lax.Precision.HIGHEST,
    )
    grad_two = expert_dx + jnp.dot(
        grad_logits, router_weight.astype(jnp.float32).T, precision=lax.Precision.HIGHEST
    )
    gain_two_grad = jnp.sum(grad_two * normed_two, axis=0)
    bias_two_grad = jnp.sum(grad_two, axis=0)
    grad_middle = grad_out + norm_back(grad_two * gain_two, normed_two, inverse_two)
    grad_branch = grad_middle.astype(jnp.bfloat16)
    grad_heads = dot(grad_branch, proj_weight, (1, 1)).astype(jnp.bfloat16)
    grad_heads = lax.all_to_all(
        grad_heads.reshape(row_count, seq_count, head_width).transpose(1, 0, 2),
        "seq",
        split_axis=0,
        concat_axis=0,
        tiled=True,
    ).reshape(length, head_width)
    proj_grad = dot(token_heads, grad_branch, (0, 0))

    early = jnp.concatenate(
        [
            proj_grad.reshape(seq_count, shard, width),
            jnp.concatenate([router_grad, gain_two_grad[None], bias_two_grad[None]], axis=0)
            .reshape(EXPERTS + 2, seq_count, shard)
            .transpose(1, 2, 0),
        ],
        axis=2,
    ).astype(jnp.bfloat16)
    early = lax.psum_scatter(early.reshape(width, width + EXPERTS + 2), "seq", scatter_dimension=0, tiled=True)
    early = lax.psum(early, "dp").astype(jnp.float32)

    grad_qkv = attend_back(qkv, doc_first[None, :], lse, heads_out, grad_heads, lows, block, block)
    grad_one_part = dot(grad_qkv, qkv_weight, (1, 1))
    gain_one_part = jnp.sum(grad_one_part * normed_all, axis=0)
    bias_one_part = jnp.sum(grad_one_part, axis=0)
    grad_one = lax.psum_scatter(
        grad_one_part.astype(jnp.bfloat16), "seq", scatter_dimension=0, tiled=True
    ).astype(jnp.float32)
    qkv_grad = dot(hidden_all, grad_qkv, (0, 0)).astype(jnp.bfloat16)
    ones = jnp.stack([gain_one_part, bias_one_part], axis=1).astype(jnp.bfloat16)
    late = jnp.concatenate([qkv_grad, ones], axis=1).reshape(seq_count, shard, 3 * head_width + 2)
    late = lax.all_to_all(late, "seq", split_axis=0, concat_axis=0, tiled=True)
    ones_sum = jnp.sum(late[:, :, 3 * head_width :].astype(jnp.float32), axis=0).astype(jnp.bfloat16)
    late = late[:, :, : 3 * head_width].reshape(seq_count, shard, 3, head_width).transpose(1, 2, 0, 3)
    late = jnp.concatenate([late.reshape(shard, 3 * width), ones_sum], axis=1)
    late = lax.psum(late, "dp").astype(jnp.float32)

    normed_one, inverse_one = normalize(inputs)
    input_grad = grad_middle + norm_back(grad_one * gain_one, normed_one, inverse_one)
    return (
        output,
        input_grad,
        late[:, 3 * width],
        late[:, 3 * width + 1],
        late[:, : 3 * width],
        early[:, :width],
        early[:, width + EXPERTS],
        early[:, width + EXPERTS + 1],
        early[:, width : width + EXPERTS],
        expert_in_grad,
        expert_out_grad,
    )


def solution(mesh):
    in_specs = (
        P(("dp", "seq"), None),
        P("dp", None),
        P(("dp", "seq"), None),
        P("seq"),
        P("seq"),
        P("seq", None),
        P("seq", None),
        P("seq"),
        P("seq"),
        P("seq", None),
        P("dp", None, "seq"),
        P("dp", "seq", None),
        P(("dp", "seq"), None),
    )
    out_specs = (
        P(("dp", "seq"), None),
        P(("dp", "seq"), None),
        P("seq"),
        P("seq"),
        P("seq", None),
        P("seq", None),
        P("seq"),
        P("seq"),
        P("seq", None),
        P("dp", None, "seq"),
        P("dp", "seq", None),
    )
    return jax.shard_map(
        per_device, mesh=mesh, in_specs=in_specs, out_specs=out_specs, check_vma=False
    )
```
